32 devices in a mesh: dp: 4 (over z), row: 2 (over core), col: 4 (over y, x).
Axes of the slice: x: 2, y: 2, z: 4, core: 2. Of those that a mesh axis runs over, the one named last changes fastest.
Arguments:
- hidden_in: bfloat16 [16384, 768], P(('dp', 'row', 'col')), may hold values from -6 to 6
- seq_lengths: int32 [32], P(('dp', 'row')), may hold values from 128 to 512, as said below
- query_weight: bfloat16 [768, 768], P('col', 'row'), may hold values from -0.21875 to 0.21875
- key_weight: bfloat16 [768, 768], P('col', 'row'), may hold values from -0.21875 to 0.21875
- value_weight: bfloat16 [768, 768], P('col', 'row'), may hold values from -0.21875 to 0.21875
- query_bias: float32 [768], P('col'), may hold values from -3 to 3
- value_bias: float32 [768], P('col'), may hold values from -3 to 3
- output_weight: bfloat16 [768, 768], P('col', 'row'), may hold values from -2 to 2
- output_bias: float32 [768], replicated, may hold values from -3 to 3
- first_gain: float32 [768], replicated, may hold values from 0.5 to 1.5
- first_shift: float32 [768], replicated, may hold values from -3 to 3
- inner_weight: bfloat16 [768, 3072], P('row', 'col'), may hold values from -0.21875 to 0.21875
- inner_bias: float32 [3072], P('col'), may hold values from -3 to 3
- outer_weight: bfloat16 [3072, 768], P('col', 'row'), may hold values from -0.109375 to 0.109375
- outer_bias: float32 [768], replicated, may hold values from -3 to 3
- second_gain: float32 [768], replicated, may hold values from 0.5 to 1.5
- second_shift: float32 [768], replicated, may hold values from -3 to 3
- cotangent: bfloat16 [16384, 768], P(('dp', 'row', 'col')), may hold values from -6 to 6
Outputs:
- result: bfloat16 [16384, 768], P(('dp', 'row', 'col'))
- grad_input: float32 [16384, 768], P(('dp', 'row', 'col'))
- grad_query_weight: float32 [768, 768], P('col', 'row')
- grad_key_weight: float32 [768, 768], P('col', 'row')
- grad_value_weight: float32 [768, 768], P('col', 'row')
- grad_query_bias: float32 [768], P('col')
- grad_value_bias: float32 [768], P('col')
- grad_output_weight: float32 [768, 768], P('col', 'row')
- grad_output_bias: float32 [768], replicated
- grad_first_gain: float32 [768], replicated
- grad_first_shift: float32 [768], replicated
- grad_inner_weight: float32 [768, 3072], P('row', 'col')
- grad_inner_bias: float32 [3072], P('col')
- grad_outer_weight: float32 [3072, 768], P('col', 'row')
- grad_outer_bias: float32 [768], replicated
- grad_second_gain: float32 [768], replicated
- grad_second_shift: float32 [768], replicated
The draws below stay inside these ranges and needn't reach their ends.
Inputs may be any that keep to these rules, and one draw needn't show every extreme that they name: `seq_lengths`: valid tokens of each sequence, counted from its start; in every draw some sequence is full.
All inputs are finite; a program needn't handle non-finite values.
Results may differ from the reference program's by a relative error of at most 0.014.
Values may be sent and summed in bfloat16 or wider, within the bound.
A program may use at most 128 MiB of HBM per device.

```python
import jax
import jax.numpy as jnp
from jax import lax

D = 768
HEADS = 12
HD = 64
FF = 3072
LEN = 512
SEQS = 32
TOKENS = 16384


def draw_seq_lengths(key, part):
    lengths = jax.random.randint(key, (SEQS,), LEN // 4, LEN + 1, dtype=jnp.int32)
    spot = jax.random.randint(jax.random.fold_in(key, 7), (), 0, SEQS, dtype=jnp.int32)
    return lengths.at[spot].set(LEN)


def level_of(stream_key, dims, split, least, largest):
    level, own = 1.0, jax.random.fold_in(stream_key, 6)
    for dim, shards_of in split:
        draws = jnp.exp(jax.random.uniform(jax.random.fold_in(own, dim), (shards_of,), jnp.float32, least / len(split), largest / len(split)))
        level = level * jnp.repeat(draws, dims[dim] // shards_of).reshape([-1 if axis == dim else 1 for axis in range(len(dims))])
    return level


def centred(rng, shape, width, limit, cuts=(), kind=jnp.bfloat16):
    level = level_of(rng, shape, cuts, -0.22, 0.18) if cuts else 1.0
    entries = jax.random.normal(rng, shape, jnp.float32) * width * level
    return jnp.minimum(jnp.maximum(entries, -limit), limit).astype(kind)


def setup_inputs(seed: int = 0) -> dict:
    splits = jax.random.split(jax.random.key(seed), 19)
    return {
        "hidden_in": centred(splits[0], (TOKENS, D), 1.0, 6.0, ((0, 32),)),
        "seq_lengths": draw_seq_lengths(jax.random.fold_in(splits[18], 71), 0),
        "query_weight": centred(splits[2], (D, D), D ** -0.5, 0.21875, ((0, 4), (1, 2))),
        "key_weight": centred(splits[3], (D, D), D ** -0.5, 0.21875, ((0, 4), (1, 2))),
        "value_weight": centred(splits[4], (D, D), D ** -0.5, 0.21875, ((0, 4), (1, 2))),
        "query_bias": centred(splits[5], (D,), 0.5, 3.0, ((0, 4),), jnp.float32),
        "value_bias": centred(splits[6], (D,), 0.5, 3.0, ((0, 4),), jnp.float32),
        "output_weight": centred(splits[7], (D, D), (max(D // 96, 2)) ** -0.5, 2.0, ((0, 4), (1, 2))),
        "output_bias": centred(splits[8], (D,), 0.5, 3.0, (), jnp.float32),
        "first_gain": jnp.clip(1.0 + 0.1 * jax.random.normal(splits[9], (D,), jnp.float32), 0.5, 1.5),
        "first_shift": centred(splits[10], (D,), 0.5, 3.0, (), jnp.float32),
        "inner_weight": centred(splits[11], (D, FF), D ** -0.5, 0.21875, ((0, 2), (1, 4))),
        "inner_bias": centred(splits[12], (FF,), 0.5, 3.0, ((0, 4),), jnp.float32),
        "outer_weight": centred(splits[13], (FF, D), FF ** -0.5, 0.109375, ((0, 4), (1, 2))),
        "outer_bias": centred(splits[14], (D,), 0.5, 3.0, (), jnp.float32),
        "second_gain": jnp.clip(1.0 + 0.1 * jax.random.normal(splits[15], (D,), jnp.float32), 0.5, 1.5),
        "second_shift": centred(splits[16], (D,), 0.5, 3.0, (), jnp.float32),
        "cotangent": centred(splits[17], (TOKENS, D), 1.0, 6.0, ((0, 32),)),
    }


@jax.custom_vjp
def low(v):
    return lax.optimization_barrier(v.astype(jnp.bfloat16)).astype(jnp.float32)

@jax.custom_vjp
def low_back(v):
    return v

def low_keep(v):
    return (low(v), None)

def low_pass(kept, grad):
    return (grad,)

def back_keep(v):
    return (v, None)

def back_low(kept, grad):
    return (low(grad),)
low.defvjp(low_keep, low_pass)
low_back.defvjp(back_keep, back_low)
EPSILON = 1e-05

def matmul(left, right):
    return jnp.dot(left, right, precision=lax.Precision.HIGHEST)

def layer_norm(resid, gain, shift):
    center = lax.optimization_barrier(jnp.mean(resid, axis=-1, keepdims=True))
    deviate = resid - center
    spread = lax.optimization_barrier(jnp.mean(deviate * deviate, axis=-1, keepdims=True))
    return deviate * lax.rsqrt(spread + EPSILON) * gain + shift

def attend_one(operands):
    queries, keys, values, length = operands
    query_heads = queries.reshape(LEN, HEADS, HD)
    key_heads = keys.reshape(LEN, HEADS, HD)
    value_heads = values.reshape(LEN, HEADS, HD)
    scores = jnp.einsum('qhd,khd->hqk', query_heads, key_heads, precision=lax.Precision.HIGHEST) * HD ** (-0.5)
    scores = low_back(scores)
    keep = jnp.arange(LEN, dtype=jnp.int32) < length
    scores = jnp.where(keep[None, None, :], scores, -1e+30)
    probs = jax.nn.softmax(scores, axis=-1)
    context = jnp.einsum('hqk,khd->qhd', low(probs), value_heads, precision=lax.Precision.HIGHEST)
    return low(low_back(context.reshape(LEN, D)))

def forward(lengths, hidden, query_weight, key_weight, value_weight, query_bias, value_bias, output_weight, output_bias, first_gain, first_shift, inner_weight, inner_bias, outer_weight, outer_bias, second_gain, second_shift):
    queries = low(low_back(matmul(hidden, query_weight.T) + query_bias))
    keys = low(low_back(matmul(hidden, key_weight.T)))
    values = low(low_back(matmul(hidden, value_weight.T) + value_bias))
    shaped = (SEQS, LEN, D)
    context = lax.map(jax.checkpoint(attend_one), (queries.reshape(shaped), keys.reshape(shaped), values.reshape(shaped), lengths))
    attended = low_back(matmul(context.reshape(TOKENS, D), output_weight))
    normed_one = layer_norm(attended + output_bias + hidden, first_gain, first_shift)
    inner = low_back(matmul(low(normed_one), inner_weight) + inner_bias)
    active = low(jax.nn.gelu(inner, approximate=False))
    outer = low_back(matmul(active, outer_weight))
    return layer_norm(outer + outer_bias + normed_one, second_gain, second_shift)

def reference(hidden_in, seq_lengths, query_weight, key_weight, value_weight, query_bias, value_bias, output_weight, output_bias, first_gain, first_shift, inner_weight, inner_bias, outer_weight, outer_bias, second_gain, second_shift, cotangent):
    params = (hidden_in, query_weight, key_weight, value_weight, query_bias, value_bias, output_weight, output_bias, first_gain, first_shift, inner_weight, inner_bias, outer_weight, outer_bias, second_gain, second_shift)
    params = tuple((p.astype(jnp.float32) for p in params))

    def closed(*values):
        return forward(seq_lengths, *values)
    output, pullback = jax.vjp(closed, *params)
    grads = pullback(cotangent.astype(jnp.float32))
    return (output.astype(jnp.bfloat16), grads[0], grads[1], grads[2], grads[3], grads[4], grads[5], grads[6], grads[7], grads[8], grads[9], grads[10], grads[11], grads[12], grads[13], grads[14], grads[15])
```

```python
from functools import partial

import jax
import jax.numpy as jnp
from jax import lax
from jax.sharding import PartitionSpec as P

HD = 64


EPSILON = 1e-05


def gather_blocks(block):
    pieces = lax.all_gather(block, "col", axis=0, tiled=False)
    return lax.all_gather(pieces, "row", axis=0, tiled=False)


def scatter_blocks(parts):
    halves = lax.psum_scatter(parts, "row", scatter_dimension=0, tiled=False)
    own = lax.psum_scatter(halves, "col", scatter_dimension=0, tiled=False)
    return lax.psum(own, "dp")


def split_blocks(value, first, second):
    rows, columns = value.shape
    shaped = value.reshape(first, rows // first, second, columns // second)
    return shaped.transpose(0, 2, 1, 3)


def dot_plain(left, right):
    return jnp.dot(left, right, preferred_element_type=jnp.float32)


def dot_first(left, right):
    return lax.dot_general(
        left, right, (((0,), (0,)), ((), ())), preferred_element_type=jnp.float32
    )


def dot_second(left, right):
    return lax.dot_general(
        left, right, (((1,), (1,)), ((), ())), preferred_element_type=jnp.float32
    )


def norm_stats(resid):
    center = jnp.mean(resid, axis=1, keepdims=True)
    deviate = resid - center
    spread = jnp.mean(deviate * deviate, axis=1, keepdims=True)
    inverse = lax.rsqrt(spread + EPSILON)
    return (deviate * inverse, inverse)


def norm_backward(grad, scaled, inverse, gain):
    weighted = grad * gain
    first_mean = jnp.mean(weighted, axis=1, keepdims=True)
    second_mean = jnp.mean(weighted * scaled, axis=1, keepdims=True)
    return inverse * (weighted - first_mean - scaled * second_mean)


def per_device(
    hidden_in,
    seq_lengths,
    query_weight,
    key_weight,
    value_weight,
    query_bias,
    value_bias,
    output_weight,
    output_bias,
    first_gain,
    first_shift,
    inner_weight,
    inner_bias,
    outer_weight,
    outer_bias,
    second_gain,
    second_shift,
    cotangent,
):
    bf16 = jnp.bfloat16
    f32 = jnp.float32
    row_size, col_size = lax.axis_size("row"), lax.axis_size("col")
    col_rank = lax.axis_index("col")
    small = gather_blocks(jnp.stack([query_weight, key_weight, value_weight, output_weight]))
    small = small.transpose(2, 1, 3, 0, 4).reshape(4, small.shape[3] * col_size, -1)
    query_full, key_full, value_full, output_full = (small[i] for i in range(4))
    inner_full = gather_blocks(inner_weight).transpose(0, 2, 1, 3)
    inner_full = inner_full.reshape(hidden_in.shape[1], -1)
    outer_full = gather_blocks(outer_weight).transpose(1, 2, 0, 3)
    outer_full = outer_full.reshape(-1, hidden_in.shape[1])
    biases = lax.all_gather(
        jnp.concatenate([query_bias, value_bias, inner_bias]), "col", axis=0, tiled=False
    )
    width = query_bias.shape[0]
    query_bias_full = biases[:, :width].reshape(-1)
    value_bias_full = biases[:, width : 2 * width].reshape(-1)
    inner_bias_full = biases[:, 2 * width :].reshape(-1)

    tokens = hidden_in.shape[0]
    seqs = seq_lengths.shape[0] // col_size
    length = tokens // seqs
    heads = query_full.shape[0] // HD
    shaped = (seqs, length, heads, HD)
    own_lengths = lax.dynamic_slice_in_dim(seq_lengths, col_rank * seqs, seqs, 0)
    positions = lax.broadcasted_iota(jnp.int32, (seqs, 1, 1, length), 3)
    keep = positions < own_lengths[:, None, None, None]
    inputs = hidden_in
    queries = (dot_second(inputs, query_full) + query_bias_full).astype(bf16)
    keys = dot_second(inputs, key_full).astype(bf16)
    values = (dot_second(inputs, value_full) + value_bias_full).astype(bf16)
    query_heads = queries.reshape(shaped)
    key_heads = keys.reshape(shaped)
    value_heads = values.reshape(shaped)
    scores = jnp.einsum(
        "sqhd,skhd->shqk", query_heads, key_heads, preferred_element_type=f32
    ) * HD ** (-0.5)
    scores = jnp.where(keep, scores, -1e30)
    top = jnp.max(scores, axis=-1, keepdims=True)
    expo = jnp.exp(scores - top)
    probs = expo / jnp.sum(expo, axis=-1, keepdims=True)
    probs_low = probs.astype(bf16)
    context = (
        jnp.einsum("shqk,skhd->sqhd", probs_low, value_heads, preferred_element_type=f32)
        .astype(bf16)
        .reshape(tokens, -1)
    )
    resid_one = dot_plain(context, output_full) + output_bias + hidden_in.astype(f32)
    scaled_one, inverse_one = norm_stats(resid_one)
    normed_one = scaled_one * first_gain + first_shift
    normed_low = normed_one.astype(bf16)
    inner = dot_plain(normed_low, inner_full) + inner_bias_full
    active, gelu_back = jax.vjp(partial(jax.nn.gelu, approximate=False), inner)
    active_low = active.astype(bf16)
    resid_two = dot_plain(active_low, outer_full) + outer_bias + normed_one
    scaled_two, inverse_two = norm_stats(resid_two)
    result = (scaled_two * second_gain + second_shift).astype(bf16)
    grad_out = cotangent.astype(f32)
    grad_second_gain = jnp.sum(grad_out * scaled_two, axis=0)
    grad_second_shift = jnp.sum(grad_out, axis=0)
    grad_two = norm_backward(grad_out, scaled_two, inverse_two, second_gain)
    grad_outer_bias = jnp.sum(grad_two, axis=0)
    grad_outer_low = grad_two.astype(bf16)
    grad_outer_weight = dot_first(active_low, grad_outer_low).astype(bf16)
    outer_own = scatter_blocks(split_blocks(grad_outer_weight, col_size, row_size).transpose(1, 0, 2, 3))
    grad_active = dot_second(grad_outer_low, outer_full)
    grad_inner = gelu_back(grad_active)[0].astype(bf16)
    grad_inner_bias = jnp.sum(grad_inner.astype(f32), axis=0)
    grad_inner_weight = dot_first(normed_low, grad_inner).astype(bf16)
    inner_own = scatter_blocks(split_blocks(grad_inner_weight, row_size, col_size))
    grad_one = dot_second(grad_inner, inner_full) + grad_two
    grad_first_gain = jnp.sum(grad_one * scaled_one, axis=0)
    grad_first_shift = jnp.sum(grad_one, axis=0)
    grad_resid = norm_backward(grad_one, scaled_one, inverse_one, first_gain)
    grad_output_bias = jnp.sum(grad_resid, axis=0)
    grad_attn_low = grad_resid.astype(bf16)
    grad_output_weight = dot_first(context, grad_attn_low)
    grad_context = dot_second(grad_attn_low, output_full).astype(bf16).reshape(shaped)
    grad_probs = jnp.einsum(
        "sqhd,skhd->shqk", grad_context, value_heads, preferred_element_type=f32
    )
    row_dot = jnp.sum(probs * grad_probs, axis=-1, keepdims=True)
    grad_scores = (probs * (grad_probs - row_dot)).astype(bf16)
    grad_queries = jnp.einsum(
        "shqk,skhd->sqhd", grad_scores, key_heads, preferred_element_type=f32
    ) * HD ** (-0.5)
    grad_queries = grad_queries.astype(bf16).reshape(tokens, -1)
    grad_keys = jnp.einsum(
        "shqk,sqhd->skhd", grad_scores, query_heads, preferred_element_type=f32
    ) * HD ** (-0.5)
    grad_keys = grad_keys.astype(bf16).reshape(tokens, -1)
    grad_values = jnp.einsum(
        "shqk,sqhd->skhd", probs_low, grad_context, preferred_element_type=f32
    )
    grad_values = grad_values.astype(bf16).reshape(tokens, -1)
    grad_query_bias = jnp.sum(grad_queries.astype(f32), axis=0)
    grad_value_bias = jnp.sum(grad_values.astype(f32), axis=0)
    small_grads = jnp.stack(
        [
            split_blocks(value.astype(bf16), col_size, row_size)
            for value in (
                dot_first(grad_queries, inputs),
                dot_first(grad_keys, inputs),
                dot_first(grad_values, inputs),
                grad_output_weight,
            )
        ],
        axis=2,
    )
    small_own = scatter_blocks(small_grads.transpose(1, 0, 2, 3, 4)).astype(f32)
    grad_input = (
        dot_plain(grad_queries, query_full)
        + dot_plain(grad_keys, key_full)
        + dot_plain(grad_values, value_full)
    ) + grad_resid
    parts = (
        grad_output_bias,
        grad_first_gain,
        grad_first_shift,
        grad_outer_bias,
        grad_second_gain,
        grad_second_shift,
        grad_query_bias,
        grad_value_bias,
        grad_inner_bias,
    )
    sums = lax.psum(jnp.concatenate(parts), ("dp", "row", "col"))
    offset, vectors = 0, []
    for part in parts:
        vectors.append(sums[offset : offset + part.shape[0]])
        offset += part.shape[0]

    def own_part(value):
        size = value.shape[0] // col_size
        return lax.dynamic_slice_in_dim(value, col_rank * size, size, 0)

    return (
        result,
        grad_input,
        small_own[0],
        small_own[1],
        small_own[2],
        own_part(vectors[6]),
        own_part(vectors[7]),
        small_own[3],
        vectors[0],
        vectors[1],
        vectors[2],
        inner_own.astype(f32),
        own_part(vectors[8]),
        outer_own.astype(f32),
        vectors[3],
        vectors[4],
        vectors[5],
    )


def solution(mesh):
    in_specs = (
        P(("dp", "row", "col"), None),
        P(("dp", "row")),
        P("col", "row"),
        P("col", "row"),
        P("col", "row"),
        P("col"),
        P("col"),
        P("col", "row"),
        P(),
        P(),
        P(),
        P("row", "col"),
        P("col"),
        P("col", "row"),
        P(),
        P(),
        P(),
        P(("dp", "row", "col"), None),
    )
    out_specs = (
        P(("dp", "row", "col"), None),
        P(("dp", "row", "col"), None),
        P("col", "row"),
        P("col", "row"),
        P("col", "row"),
        P("col"),
        P("col"),
        P("col", "row"),
        P(),
        P(),
        P(),
        P("row", "col"),
        P("col"),
        P("col", "row"),
        P(),
        P(),
        P(),
    )
    return jax.shard_map(
        per_device, mesh=mesh, in_specs=in_specs, out_specs=out_specs, check_vma=False
    )
```

```python
from functools import partial

import jax
import jax.numpy as jnp
from jax import lax
from jax.experimental import pallas as pl
from jax.experimental.pallas import tpu as pltpu
from jax.sharding import PartitionSpec as P

HD = 64


EPSILON = 1e-05


MESH = pl.DeviceIdType.MESH


def gather_kernel(flips, cols, *refs):
    count = len(flips)
    shards, fulls = refs[:count], refs[count : 2 * count]
    local, send, recv, pair_send, pair_recv = refs[2 * count :]
    me_row, me_col = lax.axis_index("row"), lax.axis_index("col")
    partner = 1 - me_row

    def place(which, row, col):
        rows, columns = shards[which].shape
        first, second = (row, col) if flips[which] else (col, row)
        return fulls[which].at[
            pl.ds(pl.multiple_of(first * rows, rows), rows),
            pl.ds(pl.multiple_of(second * columns, columns), columns),
        ]

    def to_col(which, step):
        return pltpu.make_async_remote_copy(
            src_ref=shards[which],
            dst_ref=place(which, me_row, me_col),
            send_sem=send.at[step - 1, which],
            recv_sem=recv.at[step - 1, which],
            device_id={"col": lax.rem(me_col + step, cols)},
            device_id_type=MESH,
        )

    def from_col(which, step):
        source = lax.rem(me_col + cols - step, cols)
        return pltpu.make_async_remote_copy(
            src_ref=shards[which],
            dst_ref=place(which, me_row, source),
            send_sem=send.at[step - 1, which],
            recv_sem=recv.at[step - 1, which],
            device_id={"col": lax.rem(me_col + step, cols)},
            device_id_type=MESH,
        )

    def to_pair(which, step):
        source = lax.rem(me_col + cols - step, cols)
        here = place(which, me_row, source)
        return pltpu.make_async_remote_copy(
            src_ref=shards[which] if step == 0 else here,
            dst_ref=here,
            send_sem=pair_send.at[step, which],
            recv_sem=pair_recv.at[step, which],
            device_id={"row": partner},
            device_id_type=MESH,
        )

    def from_pair(which, step):
        source = lax.rem(me_col + cols - step, cols)
        return pltpu.make_async_remote_copy(
            src_ref=shards[which],
            dst_ref=place(which, partner, source),
            send_sem=pair_send.at[step, which],
            recv_sem=pair_recv.at[step, which],
            device_id={"row": partner},
            device_id_type=MESH,
        )

    barrier = pltpu.get_barrier_semaphore()
    for step in range(1, cols):
        pl.semaphore_signal(
            barrier, inc=1, device_id={"col": lax.rem(me_col + step, cols)}, device_id_type=MESH
        )
    pl.semaphore_signal(barrier, inc=1, device_id={"row": partner}, device_id_type=MESH)
    pl.semaphore_wait(barrier, cols)
    for which in range(count):
        for step in range(1, cols):
            to_col(which, step).start()
        to_pair(which, 0).start()
        pltpu.make_async_copy(
            shards[which], place(which, me_row, me_col), local.at[which]
        ).start()
    for which in range(count):
        for step in range(1, cols):
            from_col(which, step).wait_recv()
            to_pair(which, step).start()
    for which in range(count):
        pltpu.make_async_copy(
            shards[which], place(which, me_row, me_col), local.at[which]
        ).wait()
        for step in range(cols):
            from_pair(which, step).wait_recv()
            to_pair(which, step).wait_send()
            if step:
                to_col(which, step).wait_send()


def gather_weights(collective, flips, shards):
    cols, rows = lax.axis_size("col"), lax.axis_size("row")
    fulls = []
    for shard, flip in zip(shards, flips):
        first, second = (rows, cols) if flip else (cols, rows)
        fulls.append(
            jax.ShapeDtypeStruct((shard.shape[0] * first, shard.shape[1] * second), shard.dtype)
        )
    count = len(shards)
    return pl.pallas_call(
        partial(gather_kernel, flips, cols),
        out_shape=fulls,
        in_specs=[pl.BlockSpec(memory_space=pl.ANY)] * count,
        out_specs=[pl.BlockSpec(memory_space=pl.ANY)] * count,
        scratch_shapes=[
            pltpu.SemaphoreType.DMA((count,)),
            pltpu.SemaphoreType.DMA((cols - 1, count)),
            pltpu.SemaphoreType.DMA((cols - 1, count)),
            pltpu.SemaphoreType.DMA((cols, count)),
            pltpu.SemaphoreType.DMA((cols, count)),
        ],
        compiler_params=pltpu.CompilerParams(collective_id=collective, has_side_effects=True),
    )(*shards)


def scatter_blocks(parts):
    halves = lax.psum_scatter(parts, "row", scatter_dimension=0, tiled=False)
    own = lax.psum_scatter(halves, "col", scatter_dimension=0, tiled=False)
    return lax.psum(own, "dp")


def split_blocks(value, first, second):
    rows, columns = value.shape
    shaped = value.reshape(first, rows // first, second, columns // second)
    return shaped.transpose(0, 2, 1, 3)


def dot_plain(left, right):
    return jnp.dot(left, right, preferred_element_type=jnp.float32)


def dot_first(left, right):
    return lax.dot_general(
        left, right, (((0,), (0,)), ((), ())), preferred_element_type=jnp.float32
    )


def dot_second(left, right):
    return lax.dot_general(
        left, right, (((1,), (1,)), ((), ())), preferred_element_type=jnp.float32
    )


def norm_stats(resid):
    center = jnp.mean(resid, axis=1, keepdims=True)
    deviate = resid - center
    spread = jnp.mean(deviate * deviate, axis=1, keepdims=True)
    inverse = lax.rsqrt(spread + EPSILON)
    return (deviate * inverse, inverse)


def norm_backward(grad, scaled, inverse, gain):
    weighted = grad * gain
    first_mean = jnp.mean(weighted, axis=1, keepdims=True)
    second_mean = jnp.mean(weighted * scaled, axis=1, keepdims=True)
    return inverse * (weighted - first_mean - scaled * second_mean)


def per_device(
    hidden_in,
    seq_lengths,
    query_weight,
    key_weight,
    value_weight,
    query_bias,
    value_bias,
    output_weight,
    output_bias,
    first_gain,
    first_shift,
    inner_weight,
    inner_bias,
    outer_weight,
    outer_bias,
    second_gain,
    second_shift,
    cotangent,
):
    bf16 = jnp.bfloat16
    f32 = jnp.float32
    row_size, col_size = lax.axis_size("row"), lax.axis_size("col")
    col_rank = lax.axis_index("col")
    query_full, key_full, value_full, output_full, inner_full, outer_full = gather_weights(
        0,
        (False, False, False, False, True, False),
        (query_weight, key_weight, value_weight, output_weight, inner_weight, outer_weight),
    )
    biases = lax.all_gather(
        jnp.concatenate([query_bias, value_bias, inner_bias]), "col", axis=0, tiled=False
    )
    width = query_bias.shape[0]
    query_bias_full = biases[:, :width].reshape(-1)
    value_bias_full = biases[:, width : 2 * width].reshape(-1)
    inner_bias_full = biases[:, 2 * width :].reshape(-1)

    tokens = hidden_in.shape[0]
    seqs = seq_lengths.shape[0] // col_size
    length = tokens // seqs
    heads = query_full.shape[0] // HD
    shaped = (seqs, length, heads, HD)
    own_lengths = lax.dynamic_slice_in_dim(seq_lengths, col_rank * seqs, seqs, 0)
    positions = lax.broadcasted_iota(jnp.int32, (seqs, 1, 1, length), 3)
    keep = positions < own_lengths[:, None, None, None]
    inputs = hidden_in
    queries = (dot_second(inputs, query_full) + query_bias_full).astype(bf16)
    keys = dot_second(inputs, key_full).astype(bf16)
    values = (dot_second(inputs, value_full) + value_bias_full).astype(bf16)
    query_heads = queries.reshape(shaped)
    key_heads = keys.reshape(shaped)
    value_heads = values.reshape(shaped)
    scores = jnp.einsum(
        "sqhd,skhd->shqk", query_heads, key_heads, preferred_element_type=f32
    ) * HD ** (-0.5)
    scores = jnp.where(keep, scores, -1e30)
    top = jnp.max(scores, axis=-1, keepdims=True)
    expo = jnp.exp(scores - top)
    probs = expo / jnp.sum(expo, axis=-1, keepdims=True)
    probs_low = probs.astype(bf16)
    context = (
        jnp.einsum("shqk,skhd->sqhd", probs_low, value_heads, preferred_element_type=f32)
        .astype(bf16)
        .reshape(tokens, -1)
    )
    resid_one = dot_plain(context, output_full) + output_bias + hidden_in.astype(f32)
    scaled_one, inverse_one = norm_stats(resid_one)
    normed_one = scaled_one * first_gain + first_shift
    normed_low = normed_one.astype(bf16)
    inner = dot_plain(normed_low, inner_full) + inner_bias_full
    active, gelu_back = jax.vjp(partial(jax.nn.gelu, approximate=False), inner)
    active_low = active.astype(bf16)
    resid_two = dot_plain(active_low, outer_full) + outer_bias + normed_one
    scaled_two, inverse_two = norm_stats(resid_two)
    result = (scaled_two * second_gain + second_shift).astype(bf16)
    grad_out = cotangent.astype(f32)
    grad_second_gain = jnp.sum(grad_out * scaled_two, axis=0)
    grad_second_shift = jnp.sum(grad_out, axis=0)
    grad_two = norm_backward(grad_out, scaled_two, inverse_two, second_gain)
    grad_outer_bias = jnp.sum(grad_two, axis=0)
    grad_outer_low = grad_two.astype(bf16)
    grad_outer_weight = dot_first(active_low, grad_outer_low).astype(bf16)
    outer_own = scatter_blocks(split_blocks(grad_outer_weight, col_size, row_size).transpose(1, 0, 2, 3))
    grad_active = dot_second(grad_outer_low, outer_full)
    grad_inner = gelu_back(grad_active)[0].astype(bf16)
    grad_inner_bias = jnp.sum(grad_inner.astype(f32), axis=0)
    grad_inner_weight = dot_first(normed_low, grad_inner).astype(bf16)
    inner_own = scatter_blocks(split_blocks(grad_inner_weight, row_size, col_size))
    grad_one = dot_second(grad_inner, inner_full) + grad_two
    grad_first_gain = jnp.sum(grad_one * scaled_one, axis=0)
    grad_first_shift = jnp.sum(grad_one, axis=0)
    grad_resid = norm_backward(grad_one, scaled_one, inverse_one, first_gain)
    grad_output_bias = jnp.sum(grad_resid, axis=0)
    grad_attn_low = grad_resid.astype(bf16)
    grad_output_weight = dot_first(context, grad_attn_low)
    grad_context = dot_second(grad_attn_low, output_full).astype(bf16).reshape(shaped)
    grad_probs = jnp.einsum(
        "sqhd,skhd->shqk", grad_context, value_heads, preferred_element_type=f32
    )
    row_dot = jnp.sum(probs * grad_probs, axis=-1, keepdims=True)
    grad_scores = (probs * (grad_probs - row_dot)).astype(bf16)
    grad_queries = jnp.einsum(
        "shqk,skhd->sqhd", grad_scores, key_heads, preferred_element_type=f32
    ) * HD ** (-0.5)
    grad_queries = grad_queries.astype(bf16).reshape(tokens, -1)
    grad_keys = jnp.einsum(
        "shqk,sqhd->skhd", grad_scores, query_heads, preferred_element_type=f32
    ) * HD ** (-0.5)
    grad_keys = grad_keys.astype(bf16).reshape(tokens, -1)
    grad_values = jnp.einsum(
        "shqk,sqhd->skhd", probs_low, grad_context, preferred_element_type=f32
    )
    grad_values = grad_values.astype(bf16).reshape(tokens, -1)
    grad_query_bias = jnp.sum(grad_queries.astype(f32), axis=0)
    grad_value_bias = jnp.sum(grad_values.astype(f32), axis=0)
    small_grads = jnp.stack(
        [
            split_blocks(value.astype(bf16), col_size, row_size)
            for value in (
                dot_first(grad_queries, inputs),
                dot_first(grad_keys, inputs),
                dot_first(grad_values, inputs),
                grad_output_weight,
            )
        ],
        axis=2,
    )
    small_own = scatter_blocks(small_grads.transpose(1, 0, 2, 3, 4)).astype(f32)
    grad_input = (
        dot_plain(grad_queries, query_full)
        + dot_plain(grad_keys, key_full)
        + dot_plain(grad_values, value_full)
    ) + grad_resid
    parts = (
        grad_output_bias,
        grad_first_gain,
        grad_first_shift,
        grad_outer_bias,
        grad_second_gain,
        grad_second_shift,
        grad_query_bias,
        grad_value_bias,
        grad_inner_bias,
    )
    sums = lax.psum(jnp.concatenate(parts), ("dp", "row", "col"))
    offset, vectors = 0, []
    for part in parts:
        vectors.append(sums[offset : offset + part.shape[0]])
        offset += part.shape[0]

    def own_part(value):
        size = value.shape[0] // col_size
        return lax.dynamic_slice_in_dim(value, col_rank * size, size, 0)

    return (
        result,
        grad_input,
        small_own[0],
        small_own[1],
        small_own[2],
        own_part(vectors[6]),
        own_part(vectors[7]),
        small_own[3],
        vectors[0],
        vectors[1],
        vectors[2],
        inner_own.astype(f32),
        own_part(vectors[8]),
        outer_own.astype(f32),
        vectors[3],
        vectors[4],
        vectors[5],
    )


def solution(mesh):
    in_specs = (
        P(("dp", "row", "col"), None),
        P(("dp", "row")),
        P("col", "row"),
        P("col", "row"),
        P("col", "row"),
        P("col"),
        P("col"),
        P("col", "row"),
        P(),
        P(),
        P(),
        P("row", "col"),
        P("col"),
        P("col", "row"),
        P(),
        P(),
        P(),
        P(("dp", "row", "col"), None),
    )
    out_specs = (
        P(("dp", "row", "col"), None),
        P(("dp", "row", "col"), None),
        P("col", "row"),
        P("col", "row"),
        P("col", "row"),
        P("col"),
        P("col"),
        P("col", "row"),
        P(),
        P(),
        P(),
        P("row", "col"),
        P("col"),
        P("col", "row"),
        P(),
        P(),
        P(),
    )
    return jax.shard_map(
        per_device, mesh=mesh, in_specs=in_specs, out_specs=out_specs, check_vma=False
    )
```

```python
from functools import partial

import jax
import jax.numpy as jnp
from jax import lax
from jax.experimental import pallas as pl
from jax.experimental.pallas import tpu as pltpu
from jax.sharding import PartitionSpec as P

HD = 64


EPSILON = 1e-05


MESH = pl.DeviceIdType.MESH


def gather_kernel(flips, cols, *refs):
    count = len(flips)
    shards, fulls = refs[:count], refs[count : 2 * count]
    local, send, recv, pair_send, pair_recv = refs[2 * count :]
    me_row, me_col = lax.axis_index("row"), lax.axis_index("col")
    partner = 1 - me_row

    def place(which, row, col):
        rows, columns = shards[which].shape
        first, second = (row, col) if flips[which] else (col, row)
        return fulls[which].at[
            pl.ds(pl.multiple_of(first * rows, rows), rows),
            pl.ds(pl.multiple_of(second * columns, columns), columns),
        ]

    def to_col(which, step):
        return pltpu.make_async_remote_copy(
            src_ref=shards[which],
            dst_ref=place(which, me_row, me_col),
            send_sem=send.at[step - 1, which],
            recv_sem=recv.at[step - 1, which],
            device_id={"col": lax.rem(me_col + step, cols)},
            device_id_type=MESH,
        )

    def from_col(which, step):
        source = lax.rem(me_col + cols - step, cols)
        return pltpu.make_async_remote_copy(
            src_ref=shards[which],
            dst_ref=place(which, me_row, source),
            send_sem=send.at[step - 1, which],
            recv_sem=recv.at[step - 1, which],
            device_id={"col": lax.rem(me_col + step, cols)},
            device_id_type=MESH,
        )

    def to_pair(which, step):
        source = lax.rem(me_col + cols - step, cols)
        here = place(which, me_row, source)
        return pltpu.make_async_remote_copy(
            src_ref=shards[which] if step == 0 else here,
            dst_ref=here,
            send_sem=pair_send.at[step, which],
            recv_sem=pair_recv.at[step, which],
            device_id={"row": partner},
            device_id_type=MESH,
        )

    def from_pair(which, step):
        source = lax.rem(me_col + cols - step, cols)
        return pltpu.make_async_remote_copy(
            src_ref=shards[which],
            dst_ref=place(which, partner, source),
            send_sem=pair_send.at[step, which],
            recv_sem=pair_recv.at[step, which],
            device_id={"row": partner},
            device_id_type=MESH,
        )

    barrier = pltpu.get_barrier_semaphore()
    for step in range(1, cols):
        pl.semaphore_signal(
            barrier, inc=1, device_id={"col": lax.rem(me_col + step, cols)}, device_id_type=MESH
        )
    pl.semaphore_signal(barrier, inc=1, device_id={"row": partner}, device_id_type=MESH)
    pl.semaphore_wait(barrier, cols)
    for which in range(count):
        for step in range(1, cols):
            to_col(which, step).start()
        to_pair(which, 0).start()
        pltpu.make_async_copy(
            shards[which], place(which, me_row, me_col), local.at[which]
        ).start()
    for which in range(count):
        for step in range(1, cols):
            from_col(which, step).wait_recv()
            to_pair(which, step).start()
    for which in range(count):
        pltpu.make_async_copy(
            shards[which], place(which, me_row, me_col), local.at[which]
        ).wait()
        for step in range(cols):
            from_pair(which, step).wait_recv()
            to_pair(which, step).wait_send()
            if step:
                to_col(which, step).wait_send()


def gather_weights(collective, flips, shards):
    cols, rows = lax.axis_size("col"), lax.axis_size("row")
    fulls = []
    for shard, flip in zip(shards, flips):
        first, second = (rows, cols) if flip else (cols, rows)
        fulls.append(
            jax.ShapeDtypeStruct((shard.shape[0] * first, shard.shape[1] * second), shard.dtype)
        )
    count = len(shards)
    return pl.pallas_call(
        partial(gather_kernel, flips, cols),
        out_shape=fulls,
        in_specs=[pl.BlockSpec(memory_space=pl.ANY)] * count,
        out_specs=[pl.BlockSpec(memory_space=pl.ANY)] * count,
        scratch_shapes=[
            pltpu.SemaphoreType.DMA((count,)),
            pltpu.SemaphoreType.DMA((cols - 1, count)),
            pltpu.SemaphoreType.DMA((cols - 1, count)),
            pltpu.SemaphoreType.DMA((cols, count)),
            pltpu.SemaphoreType.DMA((cols, count)),
        ],
        compiler_params=pltpu.CompilerParams(collective_id=collective, has_side_effects=True),
    )(*shards)


ROWS = 64


def scatter_kernel(flips, cols, groups, *refs):
    count, sums = len(flips), groups > 0
    total = count + 1 if sums else count
    grads, outs = refs[:count], refs[total : total + count]
    rest = refs[2 * total :]
    owns, pairs, cells = rest[:count], rest[count : 2 * count], rest[2 * count : 3 * count]
    local, pair_send, pair_recv, send, recv = rest[3 * count : 3 * count + 5]
    me_row, me_col = lax.axis_index("row"), lax.axis_index("col")
    me_dp = lax.axis_index("dp")
    partner = 1 - me_row

    def place(which, row, step):
        rows, columns = outs[which].shape
        col = lax.rem(me_col + step, cols)
        first, second = (row, col) if flips[which] else (col, row)
        return grads[which].at[
            pl.ds(pl.multiple_of(first * rows, rows), rows),
            pl.ds(pl.multiple_of(second * columns, columns), columns),
        ]

    def to_pair(which, step):
        return pltpu.make_async_remote_copy(
            src_ref=place(which, partner, step),
            dst_ref=pairs[which].at[step],
            send_sem=pair_send.at[step, which],
            recv_sem=pair_recv.at[step, which],
            device_id={"row": partner},
            device_id_type=MESH,
        )

    def to_own(which, step):
        return pltpu.make_async_copy(
            place(which, me_row, step), owns[which].at[step], local.at[step, which]
        )

    def to_col(which, step):
        return pltpu.make_async_remote_copy(
            src_ref=owns[which].at[step],
            dst_ref=cells[which].at[step - 1],
            send_sem=send.at[step - 1, which],
            recv_sem=recv.at[step - 1, which],
            device_id={"col": lax.rem(me_col + step, cols)},
            device_id_type=MESH,
        )

    barrier = pltpu.get_barrier_semaphore()
    pl.semaphore_signal(barrier, inc=1, device_id={"row": partner}, device_id_type=MESH)
    for step in range(1, cols):
        pl.semaphore_signal(
            barrier, inc=1, device_id={"col": lax.rem(me_col + step, cols)}, device_id_type=MESH
        )
    for step in range(1, groups):
        pl.semaphore_signal(
            barrier, inc=1, device_id={"dp": lax.rem(me_dp + step, groups)}, device_id_type=MESH
        )
    pl.semaphore_wait(barrier, cols + max(groups - 1, 0))

    order = [*range(1, cols), 0]
    for step in order:
        for which in range(count):
            to_pair(which, step).start()
            to_own(which, step).start()

    if sums:
        vector, answer = refs[count], refs[total + count]
        row_got, col_got, dp_got, stage, sum_send, row_sem, col_sem, dp_sem = rest[3 * count + 5 :]

        def share(source, target, axis, rank, size, sem, base):
            copies = []
            for step in range(1, size):
                copies.append(
                    pltpu.make_async_remote_copy(
                        src_ref=source,
                        dst_ref=target.at[rank],
                        send_sem=sum_send.at[base + step - 1],
                        recv_sem=sem.at[step - 1],
                        device_id={axis: lax.rem(rank + step, size)},
                        device_id_type=MESH,
                    )
                )
            for copy in copies:
                copy.start()
            target[pl.ds(rank, 1)] = source[...][None]
            for step in range(1, size):
                pltpu.make_async_remote_copy(
                    src_ref=source,
                    dst_ref=target.at[lax.rem(rank + size - step, size)],
                    send_sem=sum_send.at[base + step - 1],
                    recv_sem=sem.at[step - 1],
                    device_id={axis: lax.rem(rank + step, size)},
                    device_id_type=MESH,
                ).wait_recv()
            for copy in copies:
                copy.wait_send()
            answer_now = target[0]
            for index in range(1, size):
                answer_now = answer_now + target[index]
            return answer_now

        stage[0] = share(vector, row_got, "row", me_row, 2, row_sem, 0)
        stage[1] = share(stage.at[0], col_got, "col", me_col, cols, col_sem, 1)
        answer[...] = share(stage.at[1], dp_got, "dp", me_dp, groups, dp_sem, cols)

    for step in range(1, cols):
        for which in range(count):
            to_own(which, step).wait()
            to_pair(which, step).wait_recv()

            def add(index, carry, which=which, step=step):
                span = pl.ds(pl.multiple_of(index * ROWS, ROWS), ROWS)
                value = owns[which][step, span, :].astype(jnp.float32)
                value = value + pairs[which][step, span, :].astype(jnp.float32)
                owns[which][step, span, :] = value.astype(jnp.bfloat16)
                return carry

            lax.fori_loop(0, outs[which].shape[0] // ROWS, add, 0)
            to_col(which, step).start()
    for which in range(count):
        to_own(which, 0).wait()
        to_pair(which, 0).wait_recv()
        for step in range(1, cols):
            to_col(which, step).wait_recv()

        def finish(index, carry, which=which):
            span = pl.ds(pl.multiple_of(index * ROWS, ROWS), ROWS)
            value = owns[which][0, span, :].astype(jnp.float32)
            value = value + pairs[which][0, span, :].astype(jnp.float32)
            for step in range(1, cols):
                value = value + cells[which][step - 1, span, :].astype(jnp.float32)
            outs[which][span, :] = value.astype(outs[which].dtype)
            return carry

        lax.fori_loop(0, outs[which].shape[0] // ROWS, finish, 0)
    for which in range(count):
        for step in range(cols):
            to_pair(which, step).wait_send()
            if step:
                to_col(which, step).wait_send()


def scatter_grads(collective, flips, grads, vector=None):
    cols, rows = lax.axis_size("col"), lax.axis_size("row")
    groups = 0 if vector is None else lax.axis_size("dp")
    count = len(grads)
    shapes = []
    for grad, flip in zip(grads, flips):
        first, second = (rows, cols) if flip else (cols, rows)
        shapes.append((grad.shape[0] // first, grad.shape[1] // second))
    bf16 = jnp.bfloat16
    out_shape = [jax.ShapeDtypeStruct(shape, bf16) for shape in shapes]
    in_specs = [pl.BlockSpec(memory_space=pl.ANY)] * count
    vmem = pl.BlockSpec(memory_space=pltpu.VMEM)
    out_specs = [vmem] * count
    scratch = [pltpu.VMEM((cols, *shape), bf16) for shape in shapes] * 2
    scratch += [pltpu.VMEM((cols - 1, *shape), bf16) for shape in shapes]
    scratch += [pltpu.SemaphoreType.DMA((cols, count))] * 3
    scratch += [pltpu.SemaphoreType.DMA((cols - 1, count))] * 2
    operands = list(grads)
    if groups:
        shape = vector.shape
        operands.append(vector)
        in_specs.append(vmem)
        out_specs.append(vmem)
        out_shape.append(jax.ShapeDtypeStruct(shape, vector.dtype))
        scratch += [
            pltpu.VMEM((size, *shape), vector.dtype) for size in (rows, cols, groups, 2)
        ]
        scratch += [
            pltpu.SemaphoreType.DMA((size,))
            for size in (cols + groups - 1, rows - 1, cols - 1, groups - 1)
        ]
    return pl.pallas_call(
        partial(scatter_kernel, flips, cols, groups),
        out_shape=out_shape,
        in_specs=in_specs,
        out_specs=out_specs,
        scratch_shapes=scratch,
        compiler_params=pltpu.CompilerParams(
            collective_id=collective, has_side_effects=True, vmem_limit_bytes=40 << 20
        ),
    )(*operands)


def dot_plain(left, right):
    return jnp.dot(left, right, preferred_element_type=jnp.float32)


def dot_first(left, right):
    return lax.dot_general(
        left, right, (((0,), (0,)), ((), ())), preferred_element_type=jnp.float32
    )


def dot_second(left, right):
    return lax.dot_general(
        left, right, (((1,), (1,)), ((), ())), preferred_element_type=jnp.float32
    )


def norm_stats(resid):
    center = jnp.mean(resid, axis=1, keepdims=True)
    deviate = resid - center
    spread = jnp.mean(deviate * deviate, axis=1, keepdims=True)
    inverse = lax.rsqrt(spread + EPSILON)
    return (deviate * inverse, inverse)


def norm_backward(grad, scaled, inverse, gain):
    weighted = grad * gain
    first_mean = jnp.mean(weighted, axis=1, keepdims=True)
    second_mean = jnp.mean(weighted * scaled, axis=1, keepdims=True)
    return inverse * (weighted - first_mean - scaled * second_mean)


def per_device(
    hidden_in,
    seq_lengths,
    query_weight,
    key_weight,
    value_weight,
    query_bias,
    value_bias,
    output_weight,
    output_bias,
    first_gain,
    first_shift,
    inner_weight,
    inner_bias,
    outer_weight,
    outer_bias,
    second_gain,
    second_shift,
    cotangent,
):
    bf16 = jnp.bfloat16
    f32 = jnp.float32
    col_size = lax.axis_size("col")
    col_rank = lax.axis_index("col")
    query_full, key_full, value_full, output_full, inner_full, outer_full = gather_weights(
        0,
        (False, False, False, False, True, False),
        (query_weight, key_weight, value_weight, output_weight, inner_weight, outer_weight),
    )
    biases = lax.all_gather(
        jnp.concatenate([query_bias, value_bias, inner_bias]), "col", axis=0, tiled=False
    )
    width = query_bias.shape[0]
    query_bias_full = biases[:, :width].reshape(-1)
    value_bias_full = biases[:, width : 2 * width].reshape(-1)
    inner_bias_full = biases[:, 2 * width :].reshape(-1)

    tokens = hidden_in.shape[0]
    seqs = seq_lengths.shape[0] // col_size
    length = tokens // seqs
    heads = query_full.shape[0] // HD
    shaped = (seqs, length, heads, HD)
    own_lengths = lax.dynamic_slice_in_dim(seq_lengths, col_rank * seqs, seqs, 0)
    positions = lax.broadcasted_iota(jnp.int32, (seqs, 1, 1, length), 3)
    keep = positions < own_lengths[:, None, None, None]
    inputs = hidden_in
    queries = (dot_second(inputs, query_full) + query_bias_full).astype(bf16)
    keys = dot_second(inputs, key_full).astype(bf16)
    values = (dot_second(inputs, value_full) + value_bias_full).astype(bf16)
    query_heads = queries.reshape(shaped)
    key_heads = keys.reshape(shaped)
    value_heads = values.reshape(shaped)
    scores = jnp.einsum(
        "sqhd,skhd->shqk", query_heads, key_heads, preferred_element_type=f32
    ) * HD ** (-0.5)
    scores = jnp.where(keep, scores, -1e30)
    top = jnp.max(scores, axis=-1, keepdims=True)
    expo = jnp.exp(scores - top)
    probs = expo / jnp.sum(expo, axis=-1, keepdims=True)
    probs_low = probs.astype(bf16)
    context = (
        jnp.einsum("shqk,skhd->sqhd", probs_low, value_heads, preferred_element_type=f32)
        .astype(bf16)
        .reshape(tokens, -1)
    )
    resid_one = dot_plain(context, output_full) + output_bias + hidden_in.astype(f32)
    scaled_one, inverse_one = norm_stats(resid_one)
    normed_one = scaled_one * first_gain + first_shift
    normed_low = normed_one.astype(bf16)
    inner = dot_plain(normed_low, inner_full) + inner_bias_full
    active, gelu_back = jax.vjp(partial(jax.nn.gelu, approximate=False), inner)
    active_low = active.astype(bf16)
    resid_two = dot_plain(active_low, outer_full) + outer_bias + normed_one
    scaled_two, inverse_two = norm_stats(resid_two)
    result = (scaled_two * second_gain + second_shift).astype(bf16)
    grad_out = cotangent.astype(f32)
    grad_second_gain = jnp.sum(grad_out * scaled_two, axis=0)
    grad_second_shift = jnp.sum(grad_out, axis=0)
    grad_two = norm_backward(grad_out, scaled_two, inverse_two, second_gain)
    grad_outer_bias = jnp.sum(grad_two, axis=0)
    grad_outer_low = grad_two.astype(bf16)
    grad_outer_weight = dot_first(active_low, grad_outer_low).astype(bf16)
    grad_active = dot_second(grad_outer_low, outer_full)
    grad_inner = gelu_back(grad_active)[0].astype(bf16)
    grad_inner_bias = jnp.sum(grad_inner.astype(f32), axis=0)
    grad_inner_weight = dot_first(normed_low, grad_inner).astype(bf16)
    wide_own = scatter_grads(1, (True, False), (grad_inner_weight, grad_outer_weight))
    inner_own, outer_own = lax.psum(tuple(wide_own), "dp")
    grad_one = dot_second(grad_inner, inner_full) + grad_two
    grad_first_gain = jnp.sum(grad_one * scaled_one, axis=0)
    grad_first_shift = jnp.sum(grad_one, axis=0)
    grad_resid = norm_backward(grad_one, scaled_one, inverse_one, first_gain)
    grad_output_bias = jnp.sum(grad_resid, axis=0)
    grad_attn_low = grad_resid.astype(bf16)
    grad_output_weight = dot_first(context, grad_attn_low)
    grad_context = dot_second(grad_attn_low, output_full).astype(bf16).reshape(shaped)
    grad_probs = jnp.einsum(
        "sqhd,skhd->shqk", grad_context, value_heads, preferred_element_type=f32
    )
    row_dot = jnp.sum(probs * grad_probs, axis=-1, keepdims=True)
    grad_scores = (probs * (grad_probs - row_dot)).astype(bf16)
    grad_queries = jnp.einsum(
        "shqk,skhd->sqhd", grad_scores, key_heads, preferred_element_type=f32
    ) * HD ** (-0.5)
    grad_queries = grad_queries.astype(bf16).reshape(tokens, -1)
    grad_keys = jnp.einsum(
        "shqk,sqhd->skhd", grad_scores, query_heads, preferred_element_type=f32
    ) * HD ** (-0.5)
    grad_keys = grad_keys.astype(bf16).reshape(tokens, -1)
    grad_values = jnp.einsum(
        "shqk,sqhd->skhd", probs_low, grad_context, preferred_element_type=f32
    )
    grad_values = grad_values.astype(bf16).reshape(tokens, -1)
    grad_query_bias = jnp.sum(grad_queries.astype(f32), axis=0)
    grad_value_bias = jnp.sum(grad_values.astype(f32), axis=0)
    grad_input = (
        dot_plain(grad_queries, query_full)
        + dot_plain(grad_keys, key_full)
        + dot_plain(grad_values, value_full)
    ) + grad_resid
    parts = (
        grad_output_bias,
        grad_first_gain,
        grad_first_shift,
        grad_outer_bias,
        grad_second_gain,
        grad_second_shift,
        grad_query_bias,
        grad_value_bias,
        grad_inner_bias,
    )
    packed = jnp.concatenate(parts).reshape(-1, 128)
    *small_own, sums = scatter_grads(
        2,
        (False, False, False, False),
        tuple(
            value.astype(bf16)
            for value in (
                dot_first(grad_queries, inputs),
                dot_first(grad_keys, inputs),
                dot_first(grad_values, inputs),
                grad_output_weight,
            )
        ),
        packed,
    )
    small_own, inner_own, outer_own = lax.optimization_barrier((small_own, inner_own, outer_own))
    small_own = [value.astype(f32) for value in lax.psum(tuple(small_own), "dp")]
    sums = sums.reshape(-1)
    offset, vectors = 0, []
    for part in parts:
        vectors.append(sums[offset : offset + part.shape[0]])
        offset += part.shape[0]

    def own_part(value):
        size = value.shape[0] // col_size
        return lax.dynamic_slice_in_dim(value, col_rank * size, size, 0)

    return (
        result,
        grad_input,
        small_own[0],
        small_own[1],
        small_own[2],
        own_part(vectors[6]),
        own_part(vectors[7]),
        small_own[3],
        vectors[0],
        vectors[1],
        vectors[2],
        inner_own.astype(f32),
        own_part(vectors[8]),
        outer_own.astype(f32),
        vectors[3],
        vectors[4],
        vectors[5],
    )


def solution(mesh):
    in_specs = (
        P(("dp", "row", "col"), None),
        P(("dp", "row")),
        P("col", "row"),
        P("col", "row"),
        P("col", "row"),
        P("col"),
        P("col"),
        P("col", "row"),
        P(),
        P(),
        P(),
        P("row", "col"),
        P("col"),
        P("col", "row"),
        P(),
        P(),
        P(),
        P(("dp", "row", "col"), None),
    )
    out_specs = (
        P(("dp", "row", "col"), None),
        P(("dp", "row", "col"), None),
        P("col", "row"),
        P("col", "row"),
        P("col", "row"),
        P("col"),
        P("col"),
        P("col", "row"),
        P(),
        P(),
        P(),
        P("row", "col"),
        P("col"),
        P("col", "row"),
        P(),
        P(),
        P(),
    )
    return jax.shard_map(
        per_device, mesh=mesh, in_specs=in_specs, out_specs=out_specs, check_vma=False
    )
```
